32 devices in a mesh: rows: 8 (over z, y), grp: 4 (over x, core).
Axes of the slice: x: 2, y: 2, z: 4, core: 2. Of those that a mesh axis runs over, the one named last changes fastest.
Arguments:
- panel: float32 [8192, 256], P(('rows', 'grp')), may hold values from -6000 to 6000
- trailing: float32 [8192, 2048], P(('rows', 'grp')), may hold values from -6000 to 6000
Outputs:
- upper_panel: float32 [256, 256], replicated
- projection: float32 [256, 2048], replicated
- updated: float32 [8192, 2048], P(('rows', 'grp'))
- upper_next: float32 [256, 256], replicated
The draws below stay inside these ranges and needn't reach their ends.
All inputs are finite; a program needn't handle non-finite values.
Results may differ from the reference program's by a relative error of at most 0.00019.
Values sent between devices are 32-bit elements; how exact they have to be, the bound alone decides.
A program may use at most 128 MiB of HBM per device.

```python
import math
import jax
import jax.numpy as jnp
from jax import lax

PB = 256
TC = 2048
NROWS = 8192


def row_scale(key):
    position = jnp.arange(NROWS, dtype=jnp.float32) / max(NROWS - 1, 1)
    jitter = jnp.exp(jax.random.uniform(jax.random.fold_in(key, 11), (NROWS, 1), jnp.float32, 0.0, math.log(10.0)))
    return (3.0 ** position)[:, None] * jitter


def mixed_block(key, salt):
    coupling = jax.random.normal(jax.random.fold_in(key, salt), (PB, PB), jnp.float32)
    return jnp.eye(PB, dtype=jnp.float32) + 0.25 * coupling / math.sqrt(PB)


def panel_values(key):
    normals = jax.random.normal(jax.random.fold_in(key, 1), (NROWS, PB), jnp.float32)
    values = jnp.dot(normals, mixed_block(key, 2), precision=lax.Precision.HIGHEST)
    spread = math.log(10.0)
    column_scale = jnp.exp(jax.random.uniform(jax.random.fold_in(key, 3), (PB,), jnp.float32, 0.0, spread))
    return values * column_scale * row_scale(key)


def draw_panel(key, part):
    return panel_values(key)


def draw_trailing(key, part):
    values = panel_values(key)
    loading = jax.random.normal(jax.random.fold_in(key, 5), (PB, TC), jnp.float32) / math.sqrt(PB)
    normals = jax.random.normal(jax.random.fold_in(key, 6), (NROWS, TC), jnp.float32)
    leading = jnp.dot(normals[:, :PB], mixed_block(key, 7), precision=lax.Precision.HIGHEST)
    noise_part = jnp.concatenate([leading, normals[:, PB:]], axis=1)
    spread = math.log(10.0)
    column_scale = jnp.exp(jax.random.uniform(jax.random.fold_in(key, 8), (TC,), jnp.float32, 0.0, spread))
    noise_part = noise_part * column_scale * row_scale(key)
    return jnp.dot(values, loading, precision=lax.Precision.HIGHEST) + noise_part


def setup_inputs(seed: int = 0) -> dict:
    splits = jax.random.split(jax.random.key(seed), 3)
    panel = draw_panel(jax.random.fold_in(splits[2], 71), 0)
    trailing = draw_trailing(jax.random.fold_in(splits[2], 71), 0)
    return {"panel": panel, "trailing": trailing}


def cross(left, right):
    return lax.dot_general(left.astype(jnp.float32), right.astype(jnp.float32), (((0,), (0,)), ((), ())), precision=lax.Precision.HIGHEST, preferred_element_type=jnp.float32)

def upper_of(matrix):
    return jnp.linalg.cholesky(matrix).T

def reference(panel, trailing):
    inv_rows = 1.0 / panel.shape[0]
    width = panel.shape[1]
    upper_panel = upper_of(cross(panel, panel) * inv_rows)
    inverse = lax.linalg.triangular_solve(upper_panel, jnp.eye(width, dtype=upper_panel.dtype), left_side=True, lower=False)
    ortho_basis = jnp.dot(panel.astype(jnp.float32), inverse.astype(jnp.float32), precision=lax.Precision.HIGHEST, preferred_element_type=jnp.float32)
    projection = cross(ortho_basis, trailing) * inv_rows
    updated = trailing - jnp.dot(ortho_basis.astype(jnp.float32), projection.astype(jnp.float32), precision=lax.Precision.HIGHEST, preferred_element_type=jnp.float32)
    leading = updated[:, :width]
    upper_next = upper_of(cross(leading, leading) * inv_rows)
    return (upper_panel, projection, updated, upper_next)
```

```python
import functools

import jax
import jax.numpy as jnp
from jax import lax
from jax.experimental import pallas as pl
from jax.experimental.pallas import tpu as pltpu
from jax.sharding import PartitionSpec as P

LANES = 128
GROUP = 8


def cross(left, right):
    return lax.dot_general(
        left,
        right,
        (((0,), (0,)), ((), ())),
        precision=lax.Precision.HIGHEST,
        preferred_element_type=jnp.float32,
    )


def product(left, right):
    return jnp.dot(left, right, precision=lax.Precision.HIGHEST, preferred_element_type=jnp.float32)


def eliminate(work, order, block, with_inverse):
    chunks = order // LANES
    for start in range(0, order, block):
        stop = start + block
        live = [v for v in range(chunks) if (v + 1) * LANES > start]
        if with_inverse:
            live += [chunks + v for v in range(chunks) if v * LANES < stop]
        parts = {v: work[start:stop, v * LANES : (v + 1) * LANES] for v in live}
        done = {v: [] for v in live}
        for base in range(start, stop, GROUP):
            count = stop - base
            row_ids = lax.broadcasted_iota(jnp.int32, (count, LANES), 0)
            home, offset = divmod(base, LANES)
            cols = [
                jnp.broadcast_to(parts[home][:, offset + c : offset + c + 1], (count, LANES))
                for c in range(GROUP)
            ]
            pivots = jnp.ones((GROUP, LANES), jnp.float32)
            for k in range(GROUP):
                pivot = cols[k][k : k + 1, :]
                pivots = jnp.where(row_ids[:GROUP] == k, pivot, pivots)
                mult = jnp.where(row_ids > k, cols[k] * (1.0 / pivot), 0.0)
                for c in range(k + 1, GROUP):
                    cols[c] = cols[c] - mult * cols[c][k : k + 1, :]
                for v in live:
                    parts[v] = parts[v] - mult * parts[v][k : k + 1, :]
            scale = lax.rsqrt(pivots)
            scale = scale * (1.5 - 0.5 * pivots * scale * scale)
            for v in live:
                done[v].append(parts[v][:GROUP] * scale)
                parts[v] = parts[v][GROUP:]
        for v in live:
            work[start:stop, v * LANES : (v + 1) * LANES] = jnp.concatenate(done[v], axis=0)
        if stop < order:
            low = (stop // LANES) * LANES
            left = work[start:stop, low:order]
            high = order + (-(-stop // LANES)) * LANES if with_inverse else order
            change = cross(left, work[start:stop, low:high])
            work[stop:order, low:high] = work[stop:order, low:high] - change[stop - low :]


def eye_block(order):
    rows = lax.broadcasted_iota(jnp.int32, (order, order), 0)
    cols = lax.broadcasted_iota(jnp.int32, (order, order), 1)
    return rows, cols


def factor_kernel(with_inverse, block, matrix_ref, upper_ref, *rest):
    order = matrix_ref.shape[0]
    work = rest[-1]
    rows, cols = eye_block(order)
    work[:, :order] = matrix_ref[...]
    if with_inverse:
        work[:, order:] = jnp.where(rows == cols, 1.0, 0.0)
    eliminate(work, order, block, with_inverse)
    upper_ref[...] = jnp.where(cols >= rows, work[:, :order], 0.0)
    if with_inverse:
        rest[0][...] = jnp.where(cols <= rows, work[:, order:], 0.0)


def factor(matrix, with_inverse, block=32):
    order = matrix.shape[0]
    shape = jax.ShapeDtypeStruct((order, order), jnp.float32)
    return pl.pallas_call(
        functools.partial(factor_kernel, with_inverse, block),
        out_shape=(shape,) * (1 + with_inverse),
        in_specs=[pl.BlockSpec(memory_space=pltpu.VMEM)],
        out_specs=(pl.BlockSpec(memory_space=pltpu.VMEM),) * (1 + with_inverse),
        scratch_shapes=[pltpu.VMEM((order, order * (1 + with_inverse)), jnp.float32)],
        name="factor",
    )(matrix)


def per_device(panel, trailing):
    inv_rows = 1.0 / (panel.shape[0] * lax.axis_size(("rows", "grp")))
    width = panel.shape[1]
    gram_panel, cross_terms, gram_head = lax.psum(
        (
            cross(panel, panel),
            cross(panel, trailing),
            cross(trailing[:, :width], trailing[:, :width]),
        ),
        ("rows", "grp"),
    )
    upper_panel, lower_inv = factor(gram_panel * inv_rows, True)
    ortho_basis = product(panel, lower_inv.T)
    projection = product(lower_inv, cross_terms) * inv_rows
    updated = trailing - product(ortho_basis, projection)
    head_proj = projection[:, :width]
    (upper_next,) = factor(gram_head * inv_rows - cross(head_proj, head_proj), False)
    return (upper_panel, projection, updated, upper_next)


def solution(mesh):
    return jax.shard_map(
        per_device,
        mesh=mesh,
        in_specs=(P(("rows", "grp"), None), P(("rows", "grp"), None)),
        out_specs=(P(), P(), P(("rows", "grp"), None), P()),
        check_vma=False,
    )
```

```python
import functools

import jax
import jax.numpy as jnp
from jax import lax
from jax.experimental import pallas as pl
from jax.experimental.pallas import tpu as pltpu
from jax.sharding import PartitionSpec as P

LANES = 128
GROUP = 8


def cross(left, right):
    return lax.dot_general(
        left,
        right,
        (((0,), (0,)), ((), ())),
        precision=lax.Precision.HIGHEST,
        preferred_element_type=jnp.float32,
    )


def product(left, right):
    return jnp.dot(left, right, precision=lax.Precision.HIGHEST, preferred_element_type=jnp.float32)


def eliminate(work, order, block, with_inverse):
    chunks = order // LANES
    for start in range(0, order, block):
        stop = start + block
        live = [v for v in range(chunks) if (v + 1) * LANES > start]
        if with_inverse:
            live += [chunks + v for v in range(chunks) if v * LANES < stop]
        parts = {v: work[start:stop, v * LANES : (v + 1) * LANES] for v in live}
        done = {v: [] for v in live}
        for base in range(start, stop, GROUP):
            count = stop - base
            row_ids = lax.broadcasted_iota(jnp.int32, (count, LANES), 0)
            home, offset = divmod(base, LANES)
            cols = [
                jnp.broadcast_to(parts[home][:, offset + c : offset + c + 1], (count, LANES))
                for c in range(GROUP)
            ]
            pivots = jnp.ones((GROUP, LANES), jnp.float32)
            for k in range(GROUP):
                pivot = cols[k][k : k + 1, :]
                pivots = jnp.where(row_ids[:GROUP] == k, pivot, pivots)
                mult = jnp.where(row_ids > k, cols[k] * (1.0 / pivot), 0.0)
                for c in range(k + 1, GROUP):
                    cols[c] = cols[c] - mult * cols[c][k : k + 1, :]
                for v in live:
                    parts[v] = parts[v] - mult * parts[v][k : k + 1, :]
            scale = lax.rsqrt(pivots)
            scale = scale * (1.5 - 0.5 * pivots * scale * scale)
            for v in live:
                done[v].append(parts[v][:GROUP] * scale)
                parts[v] = parts[v][GROUP:]
        for v in live:
            work[start:stop, v * LANES : (v + 1) * LANES] = jnp.concatenate(done[v], axis=0)
        if stop < order:
            low = (stop // LANES) * LANES
            left = work[start:stop, low:order]
            high = order + (-(-stop // LANES)) * LANES if with_inverse else order
            change = cross(left, work[start:stop, low:high])
            work[stop:order, low:high] = work[stop:order, low:high] - change[stop - low :]


def eye_block(order):
    rows = lax.broadcasted_iota(jnp.int32, (order, order), 0)
    cols = lax.broadcasted_iota(jnp.int32, (order, order), 1)
    return rows, cols


def factor_kernel(with_inverse, block, matrix_ref, upper_ref, *rest):
    order = matrix_ref.shape[0]
    work = rest[-1]
    rows, cols = eye_block(order)
    work[:, :order] = matrix_ref[...]
    if with_inverse:
        work[:, order:] = jnp.where(rows == cols, 1.0, 0.0)
    eliminate(work, order, block, with_inverse)
    upper_ref[...] = jnp.where(cols >= rows, work[:, :order], 0.0)
    if with_inverse:
        rest[0][...] = jnp.where(cols <= rows, work[:, order:], 0.0)


def factor(matrix, with_inverse, block=32):
    order = matrix.shape[0]
    shape = jax.ShapeDtypeStruct((order, order), jnp.float32)
    return pl.pallas_call(
        functools.partial(factor_kernel, with_inverse, block),
        out_shape=(shape,) * (1 + with_inverse),
        in_specs=[pl.BlockSpec(memory_space=pltpu.VMEM)],
        out_specs=(pl.BlockSpec(memory_space=pltpu.VMEM),) * (1 + with_inverse),
        scratch_shapes=[pltpu.VMEM((order, order * (1 + with_inverse)), jnp.float32)],
        name="factor",
    )(matrix)


def split(value):
    high = value.astype(jnp.bfloat16)
    return high, (value - high.astype(jnp.float32)).astype(jnp.bfloat16)


def triple(left, right):
    (a, b), (c, d) = left, right
    dot = functools.partial(jnp.dot, preferred_element_type=jnp.float32)
    return dot(a, c) + (dot(a, d) + dot(b, c))


class Stream:
    def __init__(self, lo, hi, axes, sizes, order):
        self.cols = slice(lo, hi)
        self.axes, self.sizes = axes, sizes
        self.slab = order // sizes[0]
        self.part = self.slab // sizes[1]
        self.width = hi - lo

    def scratch(self):
        first, second = self.sizes
        return [
            pltpu.VMEM((first - 1, self.slab, self.width), jnp.float32),
            pltpu.VMEM((self.slab, self.width), jnp.float32),
            pltpu.VMEM((second - 1, self.part, self.width), jnp.float32),
            pltpu.SemaphoreType.DMA((4, max(self.sizes))),
            pltpu.SemaphoreType.DMA((4, max(self.sizes))),
        ]

    def bind(self, local, total, refs):
        self.local, self.total = local, total
        self.recv_first, self.sums, self.recv_second, self.send_sem, self.recv_sem = refs

    def rows(self, index, size):
        return pl.ds(pl.multiple_of(index * size, GROUP), size)

    def own(self):
        place = lax.axis_index(self.axes[0]) * self.sizes[1] + lax.axis_index(self.axes[1])
        return self.rows(place, self.part)

    def send(self, stage):
        which = (0, 1, 1, 0)[stage]
        axis, size = self.axes[which], self.sizes[which]
        me = lax.axis_index(axis)
        self.copies = []
        for k in range(1, size):
            peer = lax.rem(me + k, size)
            if stage == 0:
                src = self.local.at[self.rows(peer, self.slab), self.cols]
                dst = self.recv_first.at[k - 1]
            elif stage == 1:
                src = self.sums.at[self.rows(peer, self.part), :]
                dst = self.recv_second.at[k - 1]
            else:
                rows = self.own() if stage == 2 else self.rows(me, self.slab)
                src = dst = self.total.at[rows, self.cols]
            copy = pltpu.make_async_remote_copy(
                src_ref=src,
                dst_ref=dst,
                send_sem=self.send_sem.at[stage, k - 1],
                recv_sem=self.recv_sem.at[stage, k - 1],
                device_id={axis: peer},
                device_id_type=pl.DeviceIdType.MESH,
            )
            copy.start()
            self.copies.append(copy)

    def finish(self, stage):
        for copy in self.copies:
            copy.wait()
        if stage == 0:
            me = lax.axis_index(self.axes[0])
            value = self.local[self.rows(me, self.slab), self.cols]
            for k in range(self.sizes[0] - 1):
                value = value + self.recv_first[k]
            self.sums[...] = value
        elif stage == 1:
            me = lax.axis_index(self.axes[1])
            value = self.sums[self.rows(me, self.part), :]
            for k in range(self.sizes[1] - 1):
                value = value + self.recv_second[k]
            self.total[self.own(), self.cols] = value

    def step(self, stage):
        self.finish(stage)
        self.send(stage + 1)


def make_streams(order, width, rows, grp):
    middle = 3 * order + (width - order) // 2 // LANES * LANES
    return [
        Stream(0, order, ("grp", "rows"), (grp, rows), order),
        Stream(order, 3 * order, ("rows", "grp"), (rows, grp), order),
        Stream(3 * order, middle, ("grp", "rows"), (grp, rows), order),
        Stream(middle, 2 * order + width, ("rows", "grp"), (rows, grp), order),
    ]


def whole_kernel(rows, grp, panel_ref, trailing_ref, upper_ref, proj_ref, updated_ref, next_ref,
                 local, total, work, high_ref, low_ref, *stream_refs):
    order = panel_ref.shape[1]
    width = trailing_ref.shape[1]
    inv_rows = 1.0 / (panel_ref.shape[0] * rows * grp)
    streams = make_streams(order, width, rows, grp)
    for index, stream in enumerate(streams):
        stream.bind(local, total, stream_refs[5 * index : 5 * index + 5])
    gram, lead, left, right = streams

    barrier = pltpu.get_barrier_semaphore()
    for axis, size in (("rows", rows), ("grp", grp)):
        me = lax.axis_index(axis)
        for k in range(1, size):
            pl.semaphore_signal(barrier, inc=1, device_id={axis: lax.rem(me + k, size)},
                                device_id_type=pl.DeviceIdType.MESH)

    panel = panel_ref[...]
    head = trailing_ref[:, :order]
    local[:, :order] = cross(panel, panel)
    pl.semaphore_wait(barrier, rows + grp - 2)
    gram.send(0)
    local[:, order : 2 * order] = cross(head, head)
    local[:, 2 * order : 3 * order] = cross(panel, head)
    lead.send(0)
    high, low = split(panel.T)
    high_ref[...] = high
    low_ref[...] = low

    def cross_tiles(lo, hi):
        @pl.loop(0, (hi - lo) // LANES)
        def _(tile):
            at = pl.multiple_of(lo + tile * LANES, LANES)
            value = split(trailing_ref[:, pl.ds(at - 2 * order, LANES)])
            local[:, pl.ds(at, LANES)] = triple((high_ref[...], low_ref[...]), value)

    gram.step(0)
    cross_tiles(left.cols.start, left.cols.stop)
    left.send(0)
    gram.step(1)
    cross_tiles(right.cols.start, right.cols.stop)
    right.send(0)
    lead.step(0)
    gram.step(2)
    lead.step(1)
    gram.finish(3)
    lead.step(2)

    ids, cols = eye_block(order)
    work[:, :order] = total[:, :order] * inv_rows
    work[:, order:] = jnp.where(ids == cols, 1.0, 0.0)
    eliminate(work, order, 32, True)
    upper_ref[...] = jnp.where(cols >= ids, work[:, :order], 0.0)
    inverse = jnp.where(cols <= ids, work[:, order:], 0.0)
    work[:, order:] = inverse

    left.step(0)
    right.step(0)
    left.step(1)
    right.step(1)
    left.step(2)
    right.step(2)
    lead.finish(3)

    head_proj = product(inverse, total[:, 2 * order : 3 * order]) * inv_rows
    proj_ref[:, :order] = head_proj
    work[:, :order] = total[:, order : 2 * order] * inv_rows - cross(head_proj, head_proj)
    eliminate(work, order, 32, False)
    next_ref[...] = jnp.where(cols >= ids, work[:, :order], 0.0)

    basis = lax.dot_general(panel_ref[...], work[:, order:], (((1,), (1,)), ((), ())),
                            precision=lax.Precision.HIGHEST,
                            preferred_element_type=jnp.float32)
    high, low = split(basis)
    high_ref[...] = high
    low_ref[...] = low
    updated_ref[:, :order] = trailing_ref[:, :order] - triple((high, low), split(proj_ref[:, :order]))
    left.finish(3)
    right.finish(3)

    @pl.loop(0, (width - order) // LANES)
    def _(tile):
        at = pl.multiple_of(order + tile * LANES, LANES)
        here = pl.ds(at, LANES)
        value = split(total[:, pl.ds(2 * order + at, LANES)] * inv_rows)
        coeff = triple(split(work[:, order:]), value)
        proj_ref[:, here] = coeff
        change = triple((high_ref[...], low_ref[...]), split(coeff))
        updated_ref[:, here] = trailing_ref[:, here] - change


def fused(rows, grp, panel, trailing):
    order = panel.shape[1]
    width = trailing.shape[1]
    streams = make_streams(order, width, rows, grp)
    vmem = pl.BlockSpec(memory_space=pltpu.VMEM)
    square = jax.ShapeDtypeStruct((order, order), jnp.float32)
    scratch = [
        pltpu.VMEM((order, 2 * order + width), jnp.float32),
        pltpu.VMEM((order, 2 * order + width), jnp.float32),
        pltpu.VMEM((order, 2 * order), jnp.float32),
        pltpu.VMEM((order, panel.shape[0]), jnp.bfloat16),
        pltpu.VMEM((order, panel.shape[0]), jnp.bfloat16),
    ]
    for stream in streams:
        scratch += stream.scratch()
    return pl.pallas_call(
        functools.partial(whole_kernel, rows, grp),
        out_shape=(
            square,
            jax.ShapeDtypeStruct((order, width), jnp.float32),
            jax.ShapeDtypeStruct(trailing.shape, jnp.float32),
            square,
        ),
        in_specs=[vmem, vmem],
        out_specs=(vmem,) * 4,
        scratch_shapes=scratch,
        compiler_params=pltpu.CompilerParams(
            collective_id=0, has_side_effects=True, vmem_limit_bytes=56 * 2**20
        ),
        name="panel_step",
    )(panel, trailing)


def plain(panel, trailing):
    inv_rows = 1.0 / (panel.shape[0] * lax.axis_size(("rows", "grp")))
    width = panel.shape[1]
    gram_panel, cross_terms, gram_head = lax.psum(
        (
            cross(panel, panel),
            cross(panel, trailing),
            cross(trailing[:, :width], trailing[:, :width]),
        ),
        ("rows", "grp"),
    )
    upper_panel, lower_inv = factor(gram_panel * inv_rows, True)
    ortho_basis = product(panel, lower_inv.T)
    projection = product(lower_inv, cross_terms) * inv_rows
    updated = trailing - product(ortho_basis, projection)
    head_proj = projection[:, :width]
    (upper_next,) = factor(gram_head * inv_rows - cross(head_proj, head_proj), False)
    return (upper_panel, projection, updated, upper_next)


def solution(mesh):
    rows, grp = mesh.shape["rows"], mesh.shape["grp"]

    def per_device(panel, trailing):
        count, order = panel.shape
        width = trailing.shape[1]
        fits = order % (rows * grp * GROUP) == 0 and order % LANES == 0 and count == order
        if fits and width % LANES == 0 and width >= 2 * order and min(rows, grp) > 1:
            return fused(rows, grp, panel, trailing)
        return plain(panel, trailing)

    return jax.shard_map(
        per_device,
        mesh=mesh,
        in_specs=(P(("rows", "grp"), None), P(("rows", "grp"), None)),
        out_specs=(P(), P(), P(("rows", "grp"), None), P()),
        check_vma=False,
    )
```
